512 devices in a mesh: ctx: 32 (over z, y_lo), head: 16 (over y_hi, x, core).
Axes of the slice: x: 4, y: 8 (y_hi: 2, y_lo: 4; y = y_hi * 4 + y_lo), z: 8, core: 2. Of those that a mesh axis runs over, the one named last changes fastest.
Arguments:
- queries: bfloat16 [12288, 4096], P('ctx', 'head'), may hold values from -6 to 6
- keys: bfloat16 [12288, 4096], P('ctx', 'head'), may hold values from -6 to 6
- values: bfloat16 [12288, 4096], P('ctx', 'head'), may hold values from -6 to 6
- out_weight: bfloat16 [4096, 5120], P('head'), may hold values from -1.1953125 to 1.1953125
- neighbours: int32 [32, 7], P('ctx'), may hold values from -1 to 31, as said below
- counts: int32 [32], P('ctx'), may hold values from 1 to 7
Outputs:
- projected: bfloat16 [12288, 5120], P(('ctx', 'head'))
The draws below stay inside these ranges and needn't reach their ends.
Inputs may be any that keep to these rules, and one draw needn't show every extreme that they name: `neighbours`: for query tile g the first counts[g] entries are distinct tiles within 3 of g, g itself among them; the other entries are -1. Some tile lists 7 tiles.
All inputs are finite; a program needn't handle non-finite values.
Results may differ from the reference program's by a relative error of at most 0.019.
Values may be sent and summed in bfloat16 or wider, within the bound.
A program may use at most 64 MiB of HBM per device.

```python
import math
import jax
import jax.numpy as jnp
from jax import lax

D = 5120
HD = 128
HEADS_DEV = 2
TILE = 384
REACH = 3
HEADS = 32
NTILES = 32
TOKENS = 12288
N_HEAD = 16


def draw_queries(key, part):
    drawn = jnp.clip(1.5 * jax.random.normal(jax.random.fold_in(key, 13), (TOKENS, HEADS * HD), jnp.float32), -6.0, 6.0)
    return drawn.astype(jnp.bfloat16)


def draw_keys(key, part):
    drawn = jnp.clip(jax.random.normal(jax.random.fold_in(key, 11), (TOKENS, HEADS * HD), jnp.float32), -6.0, 6.0)
    return drawn.astype(jnp.bfloat16)


def tile_listing(key):
    window_tiles = 2 * REACH + 1
    tiles = jnp.arange(NTILES, dtype=jnp.int32)[:, None]
    offsets = jnp.arange(window_tiles, dtype=jnp.int32)[None, :] - REACH
    target = tiles + offsets
    in_range = (target >= 0) & (target < NTILES)
    slot_index = jnp.broadcast_to(jnp.arange(window_tiles, dtype=jnp.int32)[None, :], (NTILES, window_tiles))
    priority = jax.random.randint(jax.random.fold_in(key, 3), (NTILES, window_tiles), 0, 1 << 20) * window_tiles + slot_index
    priority = jnp.where(offsets == 0, (1 << 20) * window_tiles + window_tiles, priority)
    priority = jnp.where(in_range, priority, -1 - slot_index)
    unused, ranking = lax.top_k(priority, window_tiles)
    ranked_tiles = jnp.take_along_axis(target, ranking, axis=1)
    in_count = jnp.sum(in_range.astype(jnp.int32), axis=1)
    slot_count = jax.random.randint(jax.random.fold_in(key, 5), (NTILES,), 1, window_tiles + 1)
    slot_count = jnp.minimum(slot_count, in_count)
    slot_count = jnp.where(jnp.arange(NTILES, dtype=jnp.int32) == NTILES // 2, window_tiles, slot_count)
    listing = jnp.where(slot_index < slot_count[:, None], ranked_tiles, -1)
    return (listing.astype(jnp.int32), slot_count.astype(jnp.int32))


def draw_neighbours(key, part):
    listing, slot_count = tile_listing(key)
    return listing


def draw_counts(key, part):
    listing, slot_count = tile_listing(key)
    return slot_count


def shard_levels(rng, extent, shards, smallest, largest):
    loudness = 1.0
    for dim, blocks in shards:
        steps = jax.random.uniform(jax.random.fold_in(jax.random.fold_in(rng, 6), dim), (blocks,), jnp.float32, smallest / len(shards), largest / len(shards))
        loudness = loudness * jnp.repeat(jnp.exp(steps), extent[dim] // blocks).reshape((-1,) + (1,) * (len(extent) - 1 - dim))
    return loudness


def normal_values(rng, dims, scale, bound, shards=(), kind=jnp.bfloat16):
    loudness = shard_levels(rng, dims, shards, -0.22, 0.18) if shards else 1.0
    array = jax.random.normal(rng, dims, jnp.float32) * scale * loudness
    return jnp.minimum(jnp.maximum(array, -bound), bound).astype(kind)


def setup_inputs(seed: int = 0) -> dict:
    splits = jax.random.split(jax.random.key(seed), 7)
    queries = draw_queries(jax.random.fold_in(splits[6], 71), 0)
    keys = draw_keys(jax.random.fold_in(splits[6], 71), 0)
    values = normal_values(splits[2], (TOKENS, HEADS * HD), 1.0, 6.0, ((0, 32), (1, 16)))
    out_weight = normal_values(splits[3], (HEADS * HD, D), 0.2, 1.1953125, ((0, 16),))
    neighbours = draw_neighbours(jax.random.fold_in(splits[6], 71), 0)
    counts = draw_counts(jax.random.fold_in(splits[6], 71), 0)
    return {"queries": queries, "keys": keys, "values": values, "out_weight": out_weight, "neighbours": neighbours, "counts": counts}


def reference(queries, keys, values, out_weight, neighbours, counts):
    window_tiles = 2 * REACH + 1
    tile_total = counts.shape[0]
    feat_width = HEADS * HD
    padding = jnp.zeros((REACH * TILE, feat_width), keys.dtype)
    keys_padded = jnp.concatenate([padding, keys, padding], axis=0)
    values_padded = jnp.concatenate([padding, values, padding], axis=0)
    offsets = jnp.arange(window_tiles, dtype=jnp.int32) - REACH
    slot_index = jnp.arange(window_tiles, dtype=jnp.int32)
    scale = 1.0 / math.sqrt(HD)

    def one_tile(tile_index):
        target = tile_index + offsets
        listing = lax.dynamic_index_in_dim(neighbours, tile_index, 0, keepdims=False)
        slot_count = lax.dynamic_index_in_dim(counts, tile_index, 0, keepdims=False)
        member = jnp.any((listing[None, :] == target[:, None]) & (slot_index[None, :] < slot_count), axis=1)
        allowed = member & (target >= 0) & (target < tile_total)
        key_mask = jnp.repeat(allowed, TILE)
        q_tile = lax.dynamic_slice_in_dim(queries, (tile_index * TILE).astype(jnp.int32), TILE, 0)
        k_tile = lax.dynamic_slice_in_dim(keys_padded, (tile_index * TILE).astype(jnp.int32), window_tiles * TILE, 0)
        v_tile = lax.dynamic_slice_in_dim(values_padded, (tile_index * TILE).astype(jnp.int32), window_tiles * TILE, 0)
        q_heads = q_tile.reshape(TILE, HEADS, HD).astype(jnp.float32)
        k_heads = k_tile.reshape(window_tiles * TILE, HEADS, HD).astype(jnp.float32)
        v_heads = v_tile.reshape(window_tiles * TILE, HEADS, HD).astype(jnp.float32)
        scores = jnp.einsum('qhd,khd->hqk', q_heads, k_heads) * scale
        scores = jnp.where(key_mask[None, None, :], scores, -1e+30)
        row_max = lax.optimization_barrier(jnp.max(scores, axis=2, keepdims=True))
        weights = jnp.where(key_mask[None, None, :], jnp.exp(scores - row_max), 0.0)
        weight_sum = lax.optimization_barrier(jnp.sum(weights, axis=2))
        weights_low = weights.astype(jnp.bfloat16).astype(jnp.float32)
        mixed = jnp.einsum('hqk,khd->qhd', weights_low, v_heads)
        mixed = mixed / jnp.transpose(weight_sum)[:, :, None]
        return mixed.reshape(TILE, feat_width).astype(jnp.bfloat16)
    attended = lax.map(one_tile, jnp.arange(tile_total, dtype=jnp.int32)).reshape(tile_total * TILE, feat_width)
    group_width = HEADS_DEV * HD
    summed = jnp.zeros((attended.shape[0], out_weight.shape[1]), jnp.float32)
    for head_group in range(N_HEAD):
        block_cols = attended[:, head_group * group_width:(head_group + 1) * group_width]
        block_rows = out_weight[head_group * group_width:(head_group + 1) * group_width]
        partial_term = jnp.dot(block_cols, block_rows, preferred_element_type=jnp.float32)
        rounded = lax.optimization_barrier(partial_term.astype(jnp.bfloat16))
        summed = summed + rounded.astype(jnp.float32)
    return summed.astype(jnp.bfloat16)
```

```python
import functools
import math

import jax
import jax.numpy as jnp
from jax import lax
from jax.experimental import pallas as pl
from jax.experimental.pallas import tpu as pltpu
from jax.sharding import PartitionSpec as P

MESH = pl.DeviceIdType.MESH
HD = 128
TILE = 384
ROW = 4
NZ = 8
NX = 4
OWN = 24
HALF = 192
D = 5120
CHUNKS = 8
CW = D // CHUNKS
MASKED = 1e30
FACTOR = math.log2(math.e) / math.sqrt(HD)
LAG2, LAG3, LAG4 = 2, 4, 7


def body(
    q_hbm, k_hbm, v_hbm, w_hbm, nb_ref, ct_ref, out_ref,
    q_win, k_win, v_win, bias_src, bias_win, m_ref, l_ref, acc_ref, o_buf, att, w_buf,
    part, got1, got2, got3, send3, summed, send4, got4,
    s_dir, r_q, r_k, r_v, r_b, s_fwd, s_o, r_o, s_w, r_w, s1, s2, s3, s4, r1, r2, r3, r4,
):
    ctx = lax.axis_index("ctx")
    head = lax.axis_index("head")
    z, y = ctx // ROW, ctx % ROW
    yh, x, k = head // 8, (head // 2) % NX, head % 2

    def dev(zz, yy, kk):
        return {"ctx": zz * ROW + yy, "head": yh * 8 + x * 2 + kk}

    def xdev(xx):
        return {"ctx": ctx, "head": yh * 8 + xx * 2 + k}

    partner = {"ctx": ctx, "head": (1 - yh) * 8 + x * 2 + k}
    sibling = dev(z, y, 1 - k)
    right, left = (x + 1) % NX, (x + NX - 1) % NX

    w_own = pltpu.make_async_copy(w_hbm, w_buf.at[k], r_w.at[k])
    w_own.start()

    barrier = pltpu.get_barrier_semaphore()
    greeted = [sibling, xdev(right), xdev(left), partner]
    for step in range(1, ROW):
        for kk in range(2):
            greeted.append(dev(z, (y + step) % ROW, kk))
    for step in (1, NZ - 1):
        for kk in range(2):
            greeted.append(dev((z + step) % NZ, y, kk))
    for target in greeted:
        pl.semaphore_signal(barrier, inc=1, device_id=target, device_id_type=MESH)

    rows = lax.broadcasted_iota(jnp.int32, (8, HD), 0)
    bias = jnp.zeros((8, HD), jnp.float32)
    for o in range(7):
        allowed = jnp.int32(0)
        for i in range(7):
            hit = (nb_ref[0, i] == ctx + (o - 3)) & (i < ct_ref[0])
            allowed = allowed + hit.astype(jnp.int32)
        value = jnp.where(allowed > 0, jnp.float32(0), jnp.float32(MASKED))
        bias = jnp.where(rows == o, value, bias)
    bias_src[...] = bias
    m_ref[...] = jnp.full(m_ref.shape, -1e29, jnp.float32)
    l_ref[...] = jnp.zeros(l_ref.shape, jnp.float32)
    acc_ref[...] = jnp.zeros(acc_ref.shape, jnp.float32)

    pl.semaphore_wait(barrier, len(greeted))

    kd, yq = y // 2, y % 2

    def direct(i, remote):
        cols = pl.ds(i * HD, HD)
        moves = (
            (q_hbm.at[:, cols], q_win.at[yq], r_q.at[yq]),
            (bias_src, bias_win.at[yq], r_b.at[yq]),
            (k_hbm.at[:, cols], k_win.at[3 + yq], r_k.at[3 + yq]),
            (v_hbm.at[:, cols], v_win.at[3 + yq], r_v.at[3 + yq]),
        )
        out = []
        for n, (src, dst, sem) in enumerate(moves):
            if remote:
                out.append(
                    pltpu.make_async_remote_copy(
                        src, dst, s_dir.at[i, n], sem,
                        device_id=dev(z, 2 * k + i, kd), device_id_type=MESH,
                    )
                )
            else:
                out.append(pltpu.make_async_copy(src, dst, sem))
        return out

    for i in range(2):
        @pl.when(2 * k + i != y)
        def _(i=i):
            for copy in direct(i, True):
                copy.start()

    for i in range(2):
        @pl.when(2 * k + i == y)
        def _(i=i):
            for copy in direct(i, False):
                copy.start()

    w_sib = pltpu.make_async_remote_copy(
        w_hbm, w_buf.at[k], s_w, r_w.at[k], device_id=sibling, device_id_type=MESH
    )
    w_sib.start()

    def slot(a):
        return a + k * (7 - 2 * a)

    z_out, z_in = z - 1 + 2 * k, z + 1 - 2 * k
    has_out = (z_out >= 0) & (z_out < NZ)
    has_in = (z_in >= 0) & (z_in < NZ)

    def forward(a, n, b, target):
        src, dst = slot(a), slot(b)
        return [
            pltpu.make_async_remote_copy(
                win.at[src], win.at[dst], s_fwd.at[2 * n + j], sems.at[dst],
                device_id=target, device_id_type=MESH,
            )
            for j, (win, sems) in enumerate(((k_win, r_k), (v_win, r_v)))
        ]

    z_o, z_i = (z_out + NZ) % NZ, (z_in + NZ) % NZ
    plan = (
        (3, 0, 5, dev(z_o, y, 1 - k), has_out),
        (3, 1, 7, dev(z_o, y, k), has_out),
        (3, 2, 1, sibling, None),
        (4, 3, 0, dev(z_i, y, k), has_in),
        (4, 4, 6, dev(z_o, y, 1 - k), has_out),
        (4, 5, 2, sibling, None),
    )

    def arrived(sems, win, s):
        pltpu.make_async_copy(win.at[s], win.at[s], sems.at[s]).wait()

    for a in (3, 4):
        for j, (win, sems) in enumerate(((k_win, r_k), (v_win, r_v))):
            arrived(sems, win, slot(a))
            for first, n, b, target, there in plan:
                if first != a:
                    continue
                copy = forward(a, n, b, target)[j]
                if there is None:
                    copy.start()
                else:
                    pl.when(there)(copy.start)

    for i in range(2):
        arrived(r_q, q_win, i)
        arrived(r_b, bias_win, i)

    def unit(i, s):
        scores = lax.dot_general(
            q_win[i], k_win[s], (((1,), (1,)), ((), ())), preferred_element_type=jnp.float32
        )
        off = bias_win[i, pl.ds(s - i, 1), :][:, :1]
        before = m_ref[i]
        now = jnp.maximum(before, jnp.max(scores, axis=1, keepdims=True) - off)
        weights = jnp.exp2((scores - (now + off)) * FACTOR)
        alpha = jnp.exp2((before - now) * FACTOR)
        m_ref[i] = now
        l_ref[i] = alpha * l_ref[i] + jnp.sum(weights, axis=1, keepdims=True)
        acc_ref[i] = alpha * acc_ref[i] + jnp.dot(
            weights.astype(jnp.bfloat16), v_win[s], preferred_element_type=jnp.float32
        )

    def both(j, carry):
        s = slot(3 + j - (j // 4) * (2 * j - 3))

        @pl.when((j < 4) | has_out)
        def _():
            @pl.when(j >= 2)
            def _():
                arrived(r_k, k_win, s)
                arrived(r_v, v_win, s)

            unit(0, s)
            unit(1, s)

        return carry

    lax.fori_loop(0, 6, both, 0)

    def single(j, carry):
        s = slot(7 * j)
        i = j + k * (1 - 2 * j)

        @pl.when(((j == 0) & has_out) | ((j == 1) & has_in))
        def _():
            arrived(r_k, k_win, s)
            arrived(r_v, v_win, s)
            unit(i, s)

        return carry

    lax.fori_loop(0, 2, single, 0)

    def home(i, r, remote):
        src, dst = o_buf.at[i, r], att.at[y]
        if remote:
            return pltpu.make_async_remote_copy(
                src, dst, s_o.at[i, r], r_o.at[y],
                device_id=dev(z, 2 * k + i, r), device_id_type=MESH,
            )
        return pltpu.make_async_copy(src, dst, r_o.at[y])

    for i in range(2):
        mixed = acc_ref[i] * (1.0 / l_ref[i])
        for r in range(2):
            pieces = [
                mixed[OWN * (8 * h + 2 * xx + r) : OWN * (8 * h + 2 * xx + r + 1)]
                for xx in range(NX)
                for h in range(2)
            ]
            o_buf[i, r] = jnp.concatenate(pieces, axis=0).astype(jnp.bfloat16)
            here = (2 * k + i == y) & (k == r)
            pl.when(jnp.logical_not(here))(home(i, r, True).start)
            pl.when(here)(home(i, r, False).start)

    w_own.wait()
    pltpu.make_async_copy(w_buf.at[1 - k], w_buf.at[1 - k], r_w.at[1 - k]).wait()
    for j in range(ROW):
        arrived(r_o, att, j)

    low = jnp.concatenate([att[0], att[1]], axis=1)
    high = jnp.concatenate([att[2], att[3]], axis=1)

    def toward(n):
        return (right, left) if n % 2 == 0 else (left, right)

    def copy1(n):
        ahead, behind = toward(n)
        far = (x + 2) % NX
        return (
            pltpu.make_async_remote_copy(
                part.at[n, far], got1.at[n], s1.at[n], r1.at[n],
                device_id=xdev(ahead), device_id_type=MESH,
            ),
            pltpu.make_async_remote_copy(
                part.at[n, behind], got2.at[n], s2.at[n], r2.at[n],
                device_id=xdev(behind), device_id_type=MESH,
            ),
        )

    def copy3(n):
        return pltpu.make_async_remote_copy(
            send3.at[n], got3.at[n], s3.at[n], r3.at[n],
            device_id=xdev(toward(n)[0]), device_id_type=MESH,
        )

    def copy4(n):
        return pltpu.make_async_remote_copy(
            send4.at[n], got4.at[n], s4.at[n], r4.at[n],
            device_id=partner, device_id_type=MESH,
        )

    def stage1(n):
        cols = slice(n * CW, (n + 1) * CW)
        total = jnp.dot(low, w_buf[0, :, cols], preferred_element_type=jnp.float32)
        total = total + jnp.dot(high, w_buf[1, :, cols], preferred_element_type=jnp.float32)
        part[n] = total.astype(jnp.bfloat16).reshape(NX, 2 * OWN, CW)
        for copy in copy1(n):
            copy.start()

    def stage2(n):
        copy1(n)[0].wait_recv()
        own = part[n, toward(n)[0]].astype(jnp.float32)
        send3[n] = (own + got1[n].astype(jnp.float32)).astype(jnp.bfloat16)
        copy3(n).start()

    def stage3(n):
        copy1(n)[1].wait_recv()
        copy3(n).wait_recv()
        total = part[n, x].astype(jnp.float32) + got2[n].astype(jnp.float32)
        total = total + got3[n].astype(jnp.float32)
        summed[n] = total.reshape(2, OWN, CW)
        send4[n] = summed[n, 1 - yh].astype(jnp.bfloat16)
        copy4(n).start()

    def stage4(n):
        copy4(n).wait_recv()
        total = summed[n, yh] + got4[n].astype(jnp.float32)
        out_ref[:, n * CW : (n + 1) * CW] = total.astype(jnp.bfloat16)

    for step in range(CHUNKS + LAG4):
        for lag, stage in ((0, stage1), (LAG2, stage2), (LAG3, stage3), (LAG4, stage4)):
            if 0 <= step - lag < CHUNKS:
                stage(step - lag)

    for i in range(2):
        @pl.when(2 * k + i != y)
        def _(i=i):
            for copy in direct(i, True):
                copy.wait_send()
    for a, n, b, target, there in plan:
        for copy in forward(a, n, b, target):
            if there is None:
                copy.wait_send()
            else:
                pl.when(there)(copy.wait_send)
    w_sib.wait_send()
    for i in range(2):
        for r in range(2):
            here = (2 * k + i == y) & (k == r)
            pl.when(jnp.logical_not(here))(home(i, r, True).wait_send)
    for n in range(CHUNKS):
        for copy in copy1(n):
            copy.wait_send()
        copy3(n).wait_send()
        copy4(n).wait_send()


def local(queries, keys, values, out_weight, neighbours, counts):
    bf16, f32 = jnp.bfloat16, jnp.float32
    dma = pltpu.SemaphoreType.DMA
    window = pltpu.VMEM((8, TILE, HD), bf16)
    ring = pltpu.VMEM((CHUNKS, 2 * OWN, CW), bf16)
    anywhere = pl.BlockSpec(memory_space=pl.ANY)
    scalars = pl.BlockSpec(memory_space=pltpu.SMEM)
    return pl.pallas_call(
        body,
        out_shape=jax.ShapeDtypeStruct((OWN, D), bf16),
        in_specs=[anywhere] * 4 + [scalars] * 2,
        out_specs=pl.BlockSpec(memory_space=pltpu.VMEM),
        scratch_shapes=[
            pltpu.VMEM((2, TILE, HD), bf16), window, window,
            pltpu.VMEM((8, HD), f32), pltpu.VMEM((2, 8, HD), f32),
            pltpu.VMEM((2, TILE, 1), f32), pltpu.VMEM((2, TILE, 1), f32),
            pltpu.VMEM((2, TILE, HD), f32),
            pltpu.VMEM((2, 2, HALF, HD), bf16), pltpu.VMEM((ROW, HALF, HD), bf16),
            pltpu.VMEM((2, 2 * HD, D), bf16),
            pltpu.VMEM((CHUNKS, NX, 2 * OWN, CW), bf16), ring, ring, ring, ring,
            pltpu.VMEM((CHUNKS, 2, OWN, CW), f32),
            pltpu.VMEM((CHUNKS, OWN, CW), bf16), pltpu.VMEM((CHUNKS, OWN, CW), bf16),
            dma((2, 4)), dma((2,)), dma((8,)), dma((8,)), dma((2,)), dma((12,)),
            dma((2, 2)), dma((ROW,)), dma, dma((2,)),
        ] + [dma((CHUNKS,))] * 8,
        compiler_params=pltpu.CompilerParams(
            collective_id=0, has_side_effects=True, vmem_limit_bytes=48 << 20
        ),
        name="tile_attention",
    )(queries, keys, values, out_weight, neighbours, counts)


def solution(mesh):
    placed = (
        P("ctx", "head"),
        P("ctx", "head"),
        P("ctx", "head"),
        P("head", None),
        P("ctx", None),
        P("ctx"),
    )
    return jax.shard_map(
        local, mesh=mesh, in_specs=placed, out_specs=P(("ctx", "head"), None), check_vma=False
    )
```

```python
import functools
import math

import jax
import jax.numpy as jnp
from jax import lax
from jax.experimental import pallas as pl
from jax.experimental.pallas import tpu as pltpu
from jax.sharding import PartitionSpec as P

MESH = pl.DeviceIdType.MESH
HD = 128
TILE = 384
ROW = 4
NZ = 8
NX = 4
OWN = 24
HALF = 192
D = 5120
CHUNKS = 9
CW = 512
YW = 512
YH = YW // 2
XCOLS = CHUNKS * CW
MASKED = 1e30
FACTOR = math.log2(math.e) / math.sqrt(HD)
LAG2, LAG3, LAG4 = 2, 5, 9
Y2, Y3, Y4 = CHUNKS + LAG2 - 1, CHUNKS + LAG3 - 1, CHUNKS + LAG4 - 2
ORDER = (2, 1, 0, 3)


def body(
    q_hbm, k_hbm, v_hbm, w_hbm, nb_hbm, ct_ref, out_ref,
    nb_ref, q_win, k_win, v_win, bias_src, bias_win, score, weight, m_ref, l_ref, acc_ref,
    o_buf, att, w_buf,
    part, got1, got2, got3, send3, summed, send4, got4,
    part_y, send_y, got_y, half_y, got1_y, got2_y, got3_y, send3_y,
    s_dir, r_q, r_k, r_v, r_b, s_fwd, s_o, r_o, s_w, r_w, s_nb,
    s1, s2, s3, s4, r1, r2, r3, r4, s_y, r_y, s1_y, s2_y, s3_y, r1_y, r2_y, r3_y,
):
    ctx = lax.axis_index("ctx")
    head = lax.axis_index("head")
    z, y = ctx // ROW, ctx % ROW
    yh, x, k = head // 8, (head // 2) % NX, head % 2

    def dev(zz, yy, kk):
        return {"ctx": zz * ROW + yy, "head": yh * 8 + x * 2 + kk}

    def xdev(xx):
        return {"ctx": ctx, "head": yh * 8 + xx * 2 + k}

    partner = {"ctx": ctx, "head": (1 - yh) * 8 + x * 2 + k}
    sibling = dev(z, y, 1 - k)
    right, left = (x + 1) % NX, (x + NX - 1) % NX

    w_own = pltpu.make_async_copy(w_hbm, w_buf.at[k], r_w.at[k])
    w_own.start()
    listing = pltpu.make_async_copy(nb_hbm, nb_ref, s_nb)
    listing.start()

    barrier = pltpu.get_barrier_semaphore()
    greeted = [sibling, xdev(right), xdev(left), partner]
    for step in range(1, ROW):
        for kk in range(2):
            greeted.append(dev(z, (y + step) % ROW, kk))
    for step in (1, NZ - 1):
        for kk in range(2):
            greeted.append(dev((z + step) % NZ, y, kk))
    for target in greeted:
        pl.semaphore_signal(barrier, inc=1, device_id=target, device_id_type=MESH)

    z_out, z_in = z - 1 + 2 * k, z + 1 - 2 * k
    has_out = (z_out >= 0) & (z_out < NZ)
    has_in = (z_in >= 0) & (z_in < NZ)
    z_o, z_i = (z_out + NZ) % NZ, (z_in + NZ) % NZ

    def slot(a):
        return a + k * (7 - 2 * a)

    for side, tiles in ((has_out, (0, 1, 2)), (has_in, (7,))):
        @pl.when(jnp.logical_not(side))
        def _(tiles=tiles):
            for a in tiles:
                k_win[slot(a)] = jnp.zeros((TILE, HD), jnp.bfloat16)
                v_win[slot(a)] = jnp.zeros((TILE, HD), jnp.bfloat16)

    listing.wait()
    rows = lax.broadcasted_iota(jnp.int32, (8, HD), 0)
    bias = jnp.zeros((8, HD), jnp.float32)
    for o in range(7):
        allowed = jnp.int32(0)
        for i in range(7):
            hit = (nb_ref[0, i] == ctx + (o - 3)) & (i < ct_ref[0])
            allowed = allowed + hit.astype(jnp.int32)
        value = jnp.where(allowed > 0, jnp.float32(0), jnp.float32(MASKED))
        bias = jnp.where(rows == o, value, bias)
    bias_src[...] = bias
    m_ref[...] = jnp.full(m_ref.shape, -MASKED, jnp.float32)
    l_ref[...] = jnp.zeros(l_ref.shape, jnp.float32)

    pl.semaphore_wait(barrier, len(greeted))

    kd, yq = y // 2, y % 2

    def direct(i, n, remote):
        cols = pl.ds(i * HD, HD)
        src, dst, sem = (
            (q_hbm.at[:, cols], q_win.at[yq], r_q.at[yq]),
            (bias_src, bias_win.at[yq], r_b.at[yq]),
            (k_hbm.at[:, cols], k_win.at[3 + yq], r_k.at[3 + yq]),
            (v_hbm.at[:, cols], v_win.at[3 + yq], r_v.at[3 + yq]),
        )[n]
        if remote:
            return pltpu.make_async_remote_copy(
                src, dst, s_dir.at[i, n], sem,
                device_id=dev(z, 2 * k + i, kd), device_id_type=MESH,
            )
        return pltpu.make_async_copy(src, dst, sem)

    for n in ORDER:
        for i in range(2):
            pl.when(2 * k + i != y)(lambda i=i, n=n: direct(i, n, True).start())
            pl.when(2 * k + i == y)(lambda i=i, n=n: direct(i, n, False).start())

    w_sib = pltpu.make_async_remote_copy(
        w_hbm, w_buf.at[k], s_w, r_w.at[k], device_id=sibling, device_id_type=MESH
    )
    w_sib.start()

    windows = ((k_win, r_k), (v_win, r_v))
    plan = (
        (3, 0, 1, sibling, None),
        (3, 1, 5, dev(z_o, y, 1 - k), has_out),
        (4, 2, 2, sibling, None),
        (4, 3, 0, dev(z_i, y, k), has_in),
        (4, 4, 6, dev(z_o, y, 1 - k), has_out),
        (2, 5, 0, sibling, has_out),
    )

    def forward(n, b, a, target, j):
        win, sems = windows[j]
        return pltpu.make_async_remote_copy(
            win.at[slot(a)], win.at[slot(b)], s_fwd.at[j, n], sems.at[slot(b)],
            device_id=target, device_id_type=MESH,
        )

    def arrived(sems, win, s):
        pltpu.make_async_copy(win.at[s], win.at[s], sems.at[s]).wait()

    def take(a, j):
        arrived(windows[j][1], windows[j][0], slot(a))
        for source, n, b, target, there in plan:
            if source != a:
                continue
            if there is None or a == 2:
                forward(n, b, a, target, j).start()
            else:
                pl.when(there)(lambda: forward(n, b, a, target, j).start())

    def lanes(s):
        return pl.ds(pl.multiple_of(s * TILE, TILE), TILE)

    def scores(i, s):
        raw = lax.dot_general(
            q_win[i], k_win[s], (((1,), (1,)), ((), ())), preferred_element_type=jnp.float32
        )
        score[i, :, lanes(s)] = raw
        high = jnp.maximum(jnp.maximum(raw[:, :HD], raw[:, HD : 2 * HD]), raw[:, 2 * HD :])
        m_ref[i] = jnp.maximum(m_ref[i], high - bias_win[i, pl.ds(s - i, 1), :])

    def weigh(i, j):
        off = m_ref[i][:, :1] + bias_win[i, pl.ds(j, 1), :][:, :1]
        exact = jnp.exp2((score[i, :, lanes(i + j)] - off) * FACTOR)
        weight[i, :, lanes(i + j)] = exact.astype(jnp.bfloat16)
        l_ref[i] = l_ref[i] + (exact[:, :HD] + exact[:, HD : 2 * HD] + exact[:, 2 * HD :])

    def product(i, s):
        acc_ref[i] = acc_ref[i] + jnp.dot(
            weight[i, :, lanes(s)], v_win[s], preferred_element_type=jnp.float32
        )

    def mirrored(i):
        return i + k * (1 - 2 * i)

    take(3, 0)
    take(4, 0)
    for i in range(2):
        arrived(r_q, q_win, i)
        arrived(r_b, bias_win, i)

    def near_scores(j, carry):
        s = slot(3 + j)

        @pl.when(j >= 2)
        def _():
            arrived(r_k, k_win, s)

        scores(0, s)
        scores(1, s)
        return carry

    lax.fori_loop(0, 4, near_scores, 0)

    @pl.when(has_out)
    def _():
        take(2, 0)
        arrived(r_k, k_win, slot(1))

    def far_scores(j, carry):
        s = slot(2 - j)
        scores(0, s)
        scores(1, s)
        return carry

    lax.fori_loop(0, 2, far_scores, 0)

    @pl.when(has_out)
    def _():
        arrived(r_k, k_win, slot(0))

    @pl.when(has_in)
    def _():
        arrived(r_k, k_win, slot(7))

    def last_scores(j, carry):
        scores(mirrored(j), slot(7 * j))
        return carry

    lax.fori_loop(0, 2, last_scores, 0)

    take(3, 1)
    for i in range(2):
        m_ref[i] = jnp.broadcast_to(jnp.max(m_ref[i], axis=1, keepdims=True), (TILE, HD))

    def weigh_both(j, carry):
        weigh(0, j)
        weigh(1, j)
        return carry

    lax.fori_loop(0, 3, weigh_both, 0)
    take(4, 1)
    lax.fori_loop(3, 7, weigh_both, 0)

    arrived(r_v, v_win, slot(5))
    arrived(r_v, v_win, slot(6))
    first = 3 - 2 * k
    own = pl.ds(pl.multiple_of(first * TILE, TILE), ROW * TILE)
    near_v = v_win[pl.ds(first, ROW)].reshape(ROW * TILE, HD)
    for i in range(2):
        acc_ref[i] = jnp.dot(weight[i, :, own], near_v, preferred_element_type=jnp.float32)

    @pl.when(has_out)
    def _():
        take(2, 1)
        arrived(r_v, v_win, slot(1))

    def far_products(j, carry):
        s = slot(2 - j)
        product(0, s)
        product(1, s)
        return carry

    lax.fori_loop(0, 2, far_products, 0)

    @pl.when(has_out)
    def _():
        arrived(r_v, v_win, slot(0))

    @pl.when(has_in)
    def _():
        arrived(r_v, v_win, slot(7))

    def last_products(j, carry):
        product(mirrored(j), slot(7 * j))
        return carry

    lax.fori_loop(0, 2, last_products, 0)

    def home(i, r, remote):
        src, dst = o_buf.at[i, r], att.at[y]
        if remote:
            return pltpu.make_async_remote_copy(
                src, dst, s_o.at[i, r], r_o.at[y],
                device_id=dev(z, 2 * k + i, r), device_id_type=MESH,
            )
        return pltpu.make_async_copy(src, dst, r_o.at[y])

    for i in range(2):
        mixed = acc_ref[i] * (1.0 / jnp.sum(l_ref[i], axis=1, keepdims=True))
        for r in range(2):
            pieces = [
                mixed[OWN * (8 * h + 2 * xx + r) : OWN * (8 * h + 2 * xx + r + 1)]
                for xx in range(NX)
                for h in range(2)
            ]
            o_buf[i, r] = jnp.concatenate(pieces, axis=0).astype(jnp.bfloat16)
            here = (2 * k + i == y) & (k == r)
            pl.when(jnp.logical_not(here))(lambda: home(i, r, True).start())
            pl.when(here)(lambda: home(i, r, False).start())

    w_own.wait()
    pltpu.make_async_copy(w_buf.at[1 - k], w_buf.at[1 - k], r_w.at[1 - k]).wait()
    for j in range(ROW):
        arrived(r_o, att, j)

    low = jnp.concatenate([att[0], att[1]], axis=1)
    high = jnp.concatenate([att[2], att[3]], axis=1)

    def toward(n):
        return (right, left) if n % 2 == 0 else (left, right)

    def project(cols):
        total = jnp.dot(low, w_buf[0, :, cols], preferred_element_type=jnp.float32)
        return total + jnp.dot(high, w_buf[1, :, cols], preferred_element_type=jnp.float32)

    def send(src, dst, s_sem, r_sem, target):
        return pltpu.make_async_remote_copy(
            src, dst, s_sem, r_sem, device_id=target, device_id_type=MESH
        )

    far = (x + 2) % NX

    def copy1(n):
        return send(part.at[n, far], got1.at[n], s1.at[n], r1.at[n], xdev(toward(n)[0]))

    def copy2(n):
        behind = toward(n)[1]
        return send(part.at[n, behind], got2.at[n], s2.at[n], r2.at[n], xdev(behind))

    def copy3(n):
        return send(send3.at[n], got3.at[n], s3.at[n], r3.at[n], xdev(toward(n)[0]))

    def copy4(n):
        return send(send4.at[n], got4.at[n], s4.at[n], r4.at[n], partner)

    def stage1(n):
        total = project(slice(n * CW, (n + 1) * CW))
        part[n] = total.astype(jnp.bfloat16).reshape(NX, 2 * OWN, CW)
        copy1(n).start()
        copy2(n).start()

    def stage2(n):
        copy1(n).wait_recv()
        own = part[n, toward(n)[0]].astype(jnp.float32)
        send3[n] = (own + got1[n].astype(jnp.float32)).astype(jnp.bfloat16)
        copy3(n).start()

    def stage3(n):
        copy2(n).wait_recv()
        copy3(n).wait_recv()
        total = part[n, x].astype(jnp.float32) + got2[n].astype(jnp.float32)
        total = total + got3[n].astype(jnp.float32)
        summed[n] = total.reshape(2, OWN, CW)
        send4[n] = summed[n, 1 - yh].astype(jnp.bfloat16)
        copy4(n).start()

    def stage4(n):
        copy4(n).wait_recv()
        total = summed[n, yh] + got4[n].astype(jnp.float32)
        out_ref[:, n * CW : (n + 1) * CW] = total.astype(jnp.bfloat16)

    def copy_y():
        return send(send_y, got_y, s_y, r_y, partner)

    def copy1_y(h):
        return send(
            half_y.at[h, far], got1_y.at[h], s1_y.at[h], r1_y.at[h], xdev(toward(h)[0])
        )

    def copy2_y(h):
        behind = toward(h)[1]
        return send(half_y.at[h, behind], got2_y.at[h], s2_y.at[h], r2_y.at[h], xdev(behind))

    def copy3_y(h):
        return send(send3_y.at[h], got3_y.at[h], s3_y.at[h], r3_y.at[h], xdev(toward(h)[0]))

    def first_y():
        part_y[...] = project(slice(XCOLS, D)).reshape(NX, 2, OWN, YW)
        send_y[...] = part_y[:, 1 - yh].astype(jnp.bfloat16)
        copy_y().start()

    def second_y():
        copy_y().wait_recv()
        total = part_y[:, yh] + got_y[...].astype(jnp.float32)
        for h in range(2):
            half_y[h] = total[:, :, h * YH : (h + 1) * YH].astype(jnp.bfloat16)
            copy1_y(h).start()
            copy2_y(h).start()

    def third_y():
        for h in range(2):
            copy1_y(h).wait_recv()
            total = half_y[h, toward(h)[0]].astype(jnp.float32) + got1_y[h].astype(jnp.float32)
            send3_y[h] = total.astype(jnp.bfloat16)
            copy3_y(h).start()

    def fourth_y():
        for h in range(2):
            copy2_y(h).wait_recv()
            copy3_y(h).wait_recv()
            total = half_y[h, x].astype(jnp.float32) + got2_y[h].astype(jnp.float32)
            total = total + got3_y[h].astype(jnp.float32)
            out_ref[:, XCOLS + h * YH : XCOLS + (h + 1) * YH] = total.astype(jnp.bfloat16)

    extra = {0: first_y, Y2: second_y, Y3: third_y, Y4: fourth_y}
    for step in range(CHUNKS + LAG4):
        for lag, stage in ((0, stage1), (LAG2, stage2), (LAG3, stage3), (LAG4, stage4)):
            if 0 <= step - lag < CHUNKS:
                stage(step - lag)
        if step in extra:
            extra[step]()

    for n in ORDER:
        for i in range(2):
            pl.when(2 * k + i != y)(lambda i=i, n=n: direct(i, n, True).wait_send())
    for a, n, b, target, there in plan:
        for j in range(2):
            if there is None:
                forward(n, b, a, target, j).wait_send()
            else:
                pl.when(there)(lambda: forward(n, b, a, target, j).wait_send())
    w_sib.wait_send()
    for i in range(2):
        for r in range(2):
            here = (2 * k + i == y) & (k == r)
            pl.when(jnp.logical_not(here))(lambda: home(i, r, True).wait_send())
    for n in range(CHUNKS):
        for copy in (copy1, copy2, copy3, copy4):
            copy(n).wait_send()
    copy_y().wait_send()
    for h in range(2):
        for copy in (copy1_y, copy2_y, copy3_y):
            copy(h).wait_send()


def local(queries, keys, values, out_weight, neighbours, counts):
    bf16, f32 = jnp.bfloat16, jnp.float32
    vmem, dma = pltpu.VMEM, pltpu.SemaphoreType.DMA
    window = vmem((8, TILE, HD), bf16)
    per_query = vmem((2, TILE, HD), f32)
    ring = vmem((CHUNKS, 2 * OWN, CW), bf16)
    owned = vmem((CHUNKS, OWN, CW), bf16)
    ring_y = vmem((2, OWN, YH), bf16)
    anywhere = pl.BlockSpec(memory_space=pltpu.HBM)
    operands = (queries, keys, values, out_weight, neighbours)
    return pl.pallas_call(
        body,
        out_shape=jax.ShapeDtypeStruct((OWN, D), bf16),
        in_specs=[anywhere] * 5 + [pl.BlockSpec(memory_space=pltpu.SMEM)],
        out_specs=pl.BlockSpec(memory_space=vmem),
        scratch_shapes=[
            pltpu.SMEM((1, 7), jnp.int32),
            vmem((2, TILE, HD), bf16), window, window,
            vmem((8, HD), f32), vmem((2, 8, HD), f32),
            vmem((2, TILE, 8 * TILE), f32), vmem((2, TILE, 8 * TILE), bf16),
            per_query, per_query, per_query,
            vmem((2, 2, HALF, HD), bf16), vmem((ROW, HALF, HD), bf16),
            vmem((2, 2 * HD, D), bf16),
            vmem((CHUNKS, NX, 2 * OWN, CW), bf16), ring, ring, ring, ring,
            vmem((CHUNKS, 2, OWN, CW), f32), owned, owned,
            vmem((NX, 2, OWN, YW), f32), vmem((NX, OWN, YW), bf16), vmem((NX, OWN, YW), bf16),
            vmem((2, NX, OWN, YH), bf16), ring_y, ring_y, ring_y, ring_y,
            dma((2, 4)), dma((2,)), dma((8,)), dma((8,)), dma((2,)), dma((2, 6)),
            dma((2, 2)), dma((ROW,)), dma, dma((2,)), dma,
        ] + [dma((CHUNKS,))] * 8 + [dma, dma] + [dma((2,))] * 6,
        compiler_params=pltpu.CompilerParams(
            collective_id=0, has_side_effects=True, vmem_limit_bytes=48 << 20
        ),
        name="tile_attention",
    )(*[pltpu.with_memory_space_constraint(a, pltpu.HBM) for a in operands], counts)


def solution(mesh):
    placed = (
        P("ctx", "head"),
        P("ctx", "head"),
        P("ctx", "head"),
        P("head", None),
        P("ctx", None),
        P("ctx"),
    )
    return jax.shard_map(
        local, mesh=mesh, in_specs=placed, out_specs=P(("ctx", "head"), None), check_vma=False
    )
```

```python
import functools
import math

import jax
import jax.numpy as jnp
from jax import lax
from jax.experimental import pallas as pl
from jax.experimental.pallas import tpu as pltpu
from jax.sharding import PartitionSpec as P

MESH = pl.DeviceIdType.MESH
HD = 128
TILE = 384
ROW = 4
NZ = 8
NX = 4
OWN = 24
HALF = 96
D = 5120
CHUNKS = 8
CW = D // CHUNKS
MASKED = 1e30
FACTOR = math.log2(math.e) / math.sqrt(HD)
LAG2, LAG3 = 3, 6
ORDER = (2, 1, 0, 3)


def body(
    q_hbm, k_hbm, v_hbm, w_hbm, nb_hbm, ct_ref, out_ref,
    nb_ref, q_win, k_win, v_win, bias_src, bias_win, score, weight, m_ref, l_ref, acc_ref,
    o_buf, att, w_buf,
    part, got1, got2, got3, send3, send4, got4,
    s_dir, r_q, r_k, r_v, r_b, s_fwd, s_o, r_o, s_w, r_w, s_nb,
    s1, s2, s3, r1, r2, r3, s4, r4,
):
    ctx = lax.axis_index("ctx")
    head = lax.axis_index("head")
    z, y = ctx // ROW, ctx % ROW
    yh, x, k = head // 8, (head // 2) % NX, head % 2

    def dev(zz, yy, kk):
        return {"ctx": zz * ROW + yy, "head": yh * 8 + x * 2 + kk}

    def xdev(xx):
        return {"ctx": ctx, "head": yh * 8 + xx * 2 + k}

    partner = {"ctx": ctx, "head": (1 - yh) * 8 + x * 2 + k}
    sibling = dev(z, y, 1 - k)
    right, left = (x + 1) % NX, (x + NX - 1) % NX

    w_own = pltpu.make_async_copy(w_hbm, w_buf.at[k], r_w.at[k])
    w_own.start()
    listing = pltpu.make_async_copy(nb_hbm, nb_ref, s_nb)
    listing.start()

    barrier = pltpu.get_barrier_semaphore()
    greeted = [sibling, xdev(right), xdev(left), partner]
    for step in range(1, ROW):
        for kk in range(2):
            greeted.append(dev(z, (y + step) % ROW, kk))
    for step in (1, NZ - 1):
        for kk in range(2):
            greeted.append(dev((z + step) % NZ, y, kk))
    for target in greeted:
        pl.semaphore_signal(barrier, inc=1, device_id=target, device_id_type=MESH)

    z_out, z_in = z - 1 + 2 * k, z + 1 - 2 * k
    has_out = (z_out >= 0) & (z_out < NZ)
    has_in = (z_in >= 0) & (z_in < NZ)
    z_o, z_i = (z_out + NZ) % NZ, (z_in + NZ) % NZ

    def slot(a):
        return a + k * (7 - 2 * a)

    for side, tiles in ((has_out, (0, 1, 2)), (has_in, (7,))):
        @pl.when(jnp.logical_not(side))
        def _(tiles=tiles):
            for a in tiles:
                k_win[slot(a)] = jnp.zeros((TILE, HD), jnp.bfloat16)
                v_win[slot(a)] = jnp.zeros((TILE, HD), jnp.bfloat16)

    listing.wait()
    rows = lax.broadcasted_iota(jnp.int32, (8, HD), 0)
    bias = jnp.zeros((8, HD), jnp.float32)
    for o in range(7):
        allowed = jnp.int32(0)
        for i in range(7):
            hit = (nb_ref[0, i] == ctx + (o - 3)) & (i < ct_ref[0])
            allowed = allowed + hit.astype(jnp.int32)
        value = jnp.where(allowed > 0, jnp.float32(0), jnp.float32(MASKED))
        bias = jnp.where(rows == o, value, bias)
    bias_src[...] = bias
    m_ref[...] = jnp.full(m_ref.shape, -MASKED, jnp.float32)
    l_ref[...] = jnp.zeros(l_ref.shape, jnp.float32)

    pl.semaphore_wait(barrier, len(greeted))

    kd, yq = y // 2, y % 2

    def direct(i, n, remote):
        cols = pl.ds(i * HD, HD)
        src, dst, sem = (
            (q_hbm.at[:, cols], q_win.at[yq], r_q.at[yq]),
            (bias_src, bias_win.at[yq], r_b.at[yq]),
            (k_hbm.at[:, cols], k_win.at[3 + yq], r_k.at[3 + yq]),
            (v_hbm.at[:, cols], v_win.at[3 + yq], r_v.at[3 + yq]),
        )[n]
        if remote:
            return pltpu.make_async_remote_copy(
                src, dst, s_dir.at[i, n], sem,
                device_id=dev(z, 2 * k + i, kd), device_id_type=MESH,
            )
        return pltpu.make_async_copy(src, dst, sem)

    for n in ORDER:
        for i in range(2):
            pl.when(2 * k + i != y)(lambda i=i, n=n: direct(i, n, True).start())
            pl.when(2 * k + i == y)(lambda i=i, n=n: direct(i, n, False).start())

    w_sib = pltpu.make_async_remote_copy(
        w_hbm, w_buf.at[k], s_w, r_w.at[k], device_id=sibling, device_id_type=MESH
    )
    w_sib.start()

    windows = ((k_win, r_k), (v_win, r_v))
    plan = (
        (3, 0, 1, sibling, None),
        (3, 1, 5, dev(z_o, y, 1 - k), has_out),
        (4, 2, 2, sibling, None),
        (4, 3, 0, dev(z_i, y, k), has_in),
        (4, 4, 6, dev(z_o, y, 1 - k), has_out),
        (2, 5, 0, sibling, has_out),
    )

    def forward(n, b, a, target, j):
        win, sems = windows[j]
        return pltpu.make_async_remote_copy(
            win.at[slot(a)], win.at[slot(b)], s_fwd.at[j, n], sems.at[slot(b)],
            device_id=target, device_id_type=MESH,
        )

    def arrived(sems, win, s):
        pltpu.make_async_copy(win.at[s], win.at[s], sems.at[s]).wait()

    def take(a, j):
        arrived(windows[j][1], windows[j][0], slot(a))
        for source, n, b, target, there in plan:
            if source != a:
                continue
            if there is None or a == 2:
                forward(n, b, a, target, j).start()
            else:
                pl.when(there)(lambda: forward(n, b, a, target, j).start())

    def lanes(s):
        return pl.ds(pl.multiple_of(s * TILE, TILE), TILE)

    def scores(i, s):
        raw = lax.dot_general(
            q_win[i], k_win[s], (((1,), (1,)), ((), ())), preferred_element_type=jnp.float32
        )
        score[i, :, lanes(s)] = raw
        high = jnp.maximum(jnp.maximum(raw[:, :HD], raw[:, HD : 2 * HD]), raw[:, 2 * HD :])
        m_ref[i] = jnp.maximum(m_ref[i], high - bias_win[i, pl.ds(s - i, 1), :])

    def weigh(i, j):
        off = m_ref[i][:, :1] + bias_win[i, pl.ds(j, 1), :][:, :1]
        exact = jnp.exp2((score[i, :, lanes(i + j)] - off) * FACTOR)
        weight[i, :, lanes(i + j)] = exact.astype(jnp.bfloat16)
        l_ref[i] = l_ref[i] + (exact[:, :HD] + exact[:, HD : 2 * HD] + exact[:, 2 * HD :])

    def product(i, s):
        acc_ref[i] = acc_ref[i] + jnp.dot(
            weight[i, :, lanes(s)], v_win[s], preferred_element_type=jnp.float32
        )

    def mirrored(i):
        return i + k * (1 - 2 * i)

    take(3, 0)
    take(4, 0)
    for i in range(2):
        arrived(r_q, q_win, i)
        arrived(r_b, bias_win, i)

    def near_scores(j, carry):
        s = slot(3 + j)

        @pl.when(j >= 2)
        def _():
            arrived(r_k, k_win, s)

        scores(0, s)
        scores(1, s)
        return carry

    lax.fori_loop(0, 4, near_scores, 0)

    @pl.when(has_out)
    def _():
        take(2, 0)
        arrived(r_k, k_win, slot(1))

    def far_scores(j, carry):
        s = slot(2 - j)
        scores(0, s)
        scores(1, s)
        return carry

    lax.fori_loop(0, 2, far_scores, 0)

    @pl.when(has_out)
    def _():
        arrived(r_k, k_win, slot(0))

    @pl.when(has_in)
    def _():
        arrived(r_k, k_win, slot(7))

    def last_scores(j, carry):
        scores(mirrored(j), slot(7 * j))
        return carry

    lax.fori_loop(0, 2, last_scores, 0)

    take(3, 1)
    for i in range(2):
        m_ref[i] = jnp.broadcast_to(jnp.max(m_ref[i], axis=1, keepdims=True), (TILE, HD))

    def weigh_both(j, carry):
        weigh(0, j)
        weigh(1, j)
        return carry

    lax.fori_loop(0, 3, weigh_both, 0)
    take(4, 1)
    lax.fori_loop(3, 7, weigh_both, 0)

    arrived(r_v, v_win, slot(5))
    arrived(r_v, v_win, slot(6))
    first = 3 - 2 * k
    own = pl.ds(pl.multiple_of(first * TILE, TILE), ROW * TILE)
    near_v = v_win[pl.ds(first, ROW)].reshape(ROW * TILE, HD)
    for i in range(2):
        acc_ref[i] = jnp.dot(weight[i, :, own], near_v, preferred_element_type=jnp.float32)

    @pl.when(has_out)
    def _():
        take(2, 1)
        arrived(r_v, v_win, slot(1))

    def far_products(j, carry):
        s = slot(2 - j)
        product(0, s)
        product(1, s)
        return carry

    lax.fori_loop(0, 2, far_products, 0)

    @pl.when(has_out)
    def _():
        arrived(r_v, v_win, slot(0))

    @pl.when(has_in)
    def _():
        arrived(r_v, v_win, slot(7))

    def last_products(j, carry):
        product(mirrored(j), slot(7 * j))
        return carry

    lax.fori_loop(0, 2, last_products, 0)

    def side(p):
        return (1 - yh) + p * (2 * yh - 1)

    def home(p, i, r, remote):
        src, dst = o_buf.at[i, r, side(p)], att.at[p, y]
        if remote:
            return pltpu.make_async_remote_copy(
                src, dst, s_o.at[p, i, r], r_o.at[p, y],
                device_id=dev(z, 2 * k + i, r), device_id_type=MESH,
            )
        return pltpu.make_async_copy(src, dst, r_o.at[p, y])

    for i in range(2):
        mixed = acc_ref[i] * (1.0 / jnp.sum(l_ref[i], axis=1, keepdims=True))
        for r in range(2):
            for h in range(2):
                first_rows = [OWN * (8 * h + 2 * xx + r) for xx in range(NX)]
                pieces = [mixed[at : at + OWN] for at in first_rows]
                o_buf[i, r, h] = jnp.concatenate(pieces, axis=0).astype(jnp.bfloat16)
    for p in range(2):
        for i in range(2):
            for r in range(2):
                here = (2 * k + i == y) & (k == r)
                pl.when(jnp.logical_not(here))(lambda: home(p, i, r, True).start())
                pl.when(here)(lambda: home(p, i, r, False).start())

    w_own.wait()
    pltpu.make_async_copy(w_buf.at[1 - k], w_buf.at[1 - k], r_w.at[1 - k]).wait()

    def toward(c):
        return (right, left) if c % 2 == 0 else (left, right)

    def send(src, dst, s_sem, r_sem, target):
        return pltpu.make_async_remote_copy(
            src, dst, s_sem, r_sem, device_id=target, device_id_type=MESH
        )

    far = (x + 2) % NX

    def copy1(c):
        return send(part.at[c, far], got1.at[c], s1.at[c], r1.at[c], xdev(toward(c)[0]))

    def copy2(c):
        behind = toward(c)[1]
        return send(part.at[c, behind], got2.at[c], s2.at[c], r2.at[c], xdev(behind))

    def copy3(c):
        return send(send3.at[c], got3.at[c], s3.at[c], r3.at[c], xdev(toward(c)[0]))

    def copy4(n):
        return send(send4.at[n], got4.at[n], s4.at[n], r4.at[n], partner)

    inputs = []

    def stage1(c):
        p, n = c // CHUNKS, c % CHUNKS
        if n == 0:
            for j in range(ROW):
                pltpu.make_async_copy(att.at[p, j], att.at[p, j], r_o.at[p, j]).wait()
            inputs.append(
                [jnp.concatenate([att[p, j], att[p, j + 1]], axis=1) for j in (0, 2)]
            )
        low, high = inputs[p]
        cols = slice(n * CW, (n + 1) * CW)
        total = jnp.dot(low, w_buf[0, :, cols], preferred_element_type=jnp.float32)
        total = total + jnp.dot(high, w_buf[1, :, cols], preferred_element_type=jnp.float32)
        part[c] = total.reshape(NX, OWN, CW).astype(jnp.bfloat16)
        copy1(c).start()
        copy2(c).start()

    def stage2(c):
        copy1(c).wait_recv()
        own = part[c, toward(c)[0]].astype(jnp.float32)
        send3[c] = (own + got1[c].astype(jnp.float32)).astype(jnp.bfloat16)
        copy3(c).start()

    def stage3(c):
        p, n = c // CHUNKS, c % CHUNKS
        copy2(c).wait_recv()
        copy3(c).wait_recv()
        total = part[c, x].astype(jnp.float32) + got2[c].astype(jnp.float32)
        total = total + got3[c].astype(jnp.float32)
        if p == 0:
            send4[n] = total.astype(jnp.bfloat16)
            copy4(n).start()
        else:
            copy4(n).wait_recv()
            total = total + got4[n].astype(jnp.float32)
            out_ref[:, n * CW : (n + 1) * CW] = total.astype(jnp.bfloat16)

    for step in range(2 * CHUNKS + LAG3):
        for lag, stage in ((0, stage1), (LAG2, stage2), (LAG3, stage3)):
            if 0 <= step - lag < 2 * CHUNKS:
                stage(step - lag)

    for n in ORDER:
        for i in range(2):
            pl.when(2 * k + i != y)(lambda i=i, n=n: direct(i, n, True).wait_send())
    for a, n, b, target, there in plan:
        for j in range(2):
            if there is None:
                forward(n, b, a, target, j).wait_send()
            else:
                pl.when(there)(lambda: forward(n, b, a, target, j).wait_send())
    w_sib.wait_send()
    for p in range(2):
        for i in range(2):
            for r in range(2):
                here = (2 * k + i == y) & (k == r)
                pl.when(jnp.logical_not(here))(lambda: home(p, i, r, True).wait_send())
    for c in range(2 * CHUNKS):
        for copy in (copy1, copy2, copy3):
            copy(c).wait_send()
    for n in range(CHUNKS):
        copy4(n).wait_send()


def local(queries, keys, values, out_weight, neighbours, counts):
    bf16, f32 = jnp.bfloat16, jnp.float32
    vmem, dma = pltpu.VMEM, pltpu.SemaphoreType.DMA
    window = vmem((8, TILE, HD), bf16)
    per_query = vmem((2, TILE, HD), f32)
    ring = vmem((2 * CHUNKS, OWN, CW), bf16)
    owned = vmem((CHUNKS, OWN, CW), bf16)
    anywhere = pl.BlockSpec(memory_space=pltpu.HBM)
    operands = (queries, keys, values, out_weight, neighbours)
    return pl.pallas_call(
        body,
        out_shape=jax.ShapeDtypeStruct((OWN, D), bf16),
        in_specs=[anywhere] * 5 + [pl.BlockSpec(memory_space=pltpu.SMEM)],
        out_specs=pl.BlockSpec(memory_space=vmem),
        scratch_shapes=[
            pltpu.SMEM((1, 7), jnp.int32),
            vmem((2, TILE, HD), bf16), window, window,
            vmem((8, HD), f32), vmem((2, 8, HD), f32),
            vmem((2, TILE, 8 * TILE), f32), vmem((2, TILE, 8 * TILE), bf16),
            per_query, per_query, per_query,
            vmem((2, 2, 2, HALF, HD), bf16), vmem((2, ROW, HALF, HD), bf16),
            vmem((2, 2 * HD, D), bf16),
            vmem((2 * CHUNKS, NX, OWN, CW), bf16), ring, ring, ring, ring, owned, owned,
            dma((2, 4)), dma((2,)), dma((8,)), dma((8,)), dma((2,)), dma((2, 6)),
            dma((2, 2, 2)), dma((2, ROW)), dma, dma((2,)), dma,
        ] + [dma((2 * CHUNKS,))] * 6 + [dma((CHUNKS,))] * 2,
        compiler_params=pltpu.CompilerParams(
            collective_id=0, has_side_effects=True, vmem_limit_bytes=48 << 20
        ),
        name="tile_attention",
    )(*[pltpu.with_memory_space_constraint(a, pltpu.HBM) for a in operands], counts)


def solution(mesh):
    placed = (
        P("ctx", "head"),
        P("ctx", "head"),
        P("ctx", "head"),
        P("head", None),
        P("ctx", None),
        P("ctx"),
    )
    return jax.shard_map(
        local, mesh=mesh, in_specs=placed, out_specs=P(("ctx", "head"), None), check_vma=False
    )
```

```python
import functools
import math

import jax
import jax.numpy as jnp
from jax import lax
from jax.experimental import pallas as pl
from jax.experimental.pallas import tpu as pltpu
from jax.sharding import PartitionSpec as P

MESH = pl.DeviceIdType.MESH
HD = 128
TILE = 384
ROW = 4
NZ = 8
NX = 4
OWN = 24
HALF = 96
D = 5120
WIDTHS = (640,) * 8
MASKED = 1e30
FACTOR = math.log2(math.e) / math.sqrt(HD)
LAG2, LAG3 = 3, 6
ORDER = (2, 1, 0, 3)


def body(
    q_hbm, k_hbm, v_hbm, w_hbm, nb_hbm, ct_ref, out_ref,
    nb_ref, q_win, k_win, v_win, bias_src, bias_win, score, weight, m_ref, l_ref, acc_ref,
    o_buf, att, w_buf,
    part, got1, got2, got3, send3, send4, got4,
    s_dir, r_q, r_k, r_v, r_b, s_fwd, s_o, r_o, s_w, r_w, s_nb,
    s1, s2, s3, s4, r1, r2, r3, r4,
):
    ctx = lax.axis_index("ctx")
    head = lax.axis_index("head")
    z, y = ctx // ROW, ctx % ROW
    yh, x, k = head // 8, (head // 2) % NX, head % 2

    def dev(zz, yy, kk):
        return {"ctx": zz * ROW + yy, "head": yh * 8 + x * 2 + kk}

    def xdev(xx):
        return {"ctx": ctx, "head": yh * 8 + xx * 2 + k}

    partner = {"ctx": ctx, "head": (1 - yh) * 8 + x * 2 + k}
    sibling = dev(z, y, 1 - k)
    right, left = (x + 1) % NX, (x + NX - 1) % NX

    w_own = pltpu.make_async_copy(w_hbm, w_buf.at[k], r_w.at[k])
    w_own.start()
    listing = pltpu.make_async_copy(nb_hbm, nb_ref, s_nb)
    listing.start()

    barrier = pltpu.get_barrier_semaphore()
    greeted = [sibling, xdev(right), xdev(left), partner]
    for step in range(1, ROW):
        for kk in range(2):
            greeted.append(dev(z, (y + step) % ROW, kk))
    for step in (1, NZ - 1):
        for kk in range(2):
            greeted.append(dev((z + step) % NZ, y, kk))
    for target in greeted:
        pl.semaphore_signal(barrier, inc=1, device_id=target, device_id_type=MESH)

    z_out, z_in = z - 1 + 2 * k, z + 1 - 2 * k
    has_out = (z_out >= 0) & (z_out < NZ)
    has_in = (z_in >= 0) & (z_in < NZ)
    z_o, z_i = (z_out + NZ) % NZ, (z_in + NZ) % NZ

    def slot(a):
        return a + k * (7 - 2 * a)

    for side, tiles in ((has_out, (0, 1, 2)), (has_in, (7,))):
        @pl.when(jnp.logical_not(side))
        def _(tiles=tiles):
            for a in tiles:
                k_win[slot(a)] = jnp.zeros((TILE, HD), jnp.bfloat16)
                v_win[slot(a)] = jnp.zeros((TILE, HD), jnp.bfloat16)

    listing.wait()
    rows = lax.broadcasted_iota(jnp.int32, (8, HD), 0)
    bias = jnp.zeros((8, HD), jnp.float32)
    for o in range(7):
        allowed = jnp.int32(0)
        for i in range(7):
            hit = (nb_ref[0, i] == ctx + (o - 3)) & (i < ct_ref[0])
            allowed = allowed + hit.astype(jnp.int32)
        value = jnp.where(allowed > 0, jnp.float32(0), jnp.float32(MASKED))
        bias = jnp.where(rows == o, value, bias)
    bias_src[...] = bias
    m_ref[...] = jnp.full(m_ref.shape, -MASKED, jnp.float32)
    l_ref[...] = jnp.zeros(l_ref.shape, jnp.float32)

    pl.semaphore_wait(barrier, len(greeted))

    kd, yq = y // 2, y % 2

    def direct(i, n, remote):
        cols = pl.ds(i * HD, HD)
        src, dst, sem = (
            (q_hbm.at[:, cols], q_win.at[yq], r_q.at[yq]),
            (bias_src, bias_win.at[yq], r_b.at[yq]),
            (k_hbm.at[:, cols], k_win.at[3 + yq], r_k.at[3 + yq]),
            (v_hbm.at[:, cols], v_win.at[3 + yq], r_v.at[3 + yq]),
        )[n]
        if remote:
            return pltpu.make_async_remote_copy(
                src, dst, s_dir.at[i, n], sem,
                device_id=dev(z, 2 * k + i, kd), device_id_type=MESH,
            )
        return pltpu.make_async_copy(src, dst, sem)

    w_sib = pltpu.make_async_remote_copy(
        w_hbm, w_buf.at[k], s_w, r_w.at[k], device_id=sibling, device_id_type=MESH
    )

    for n in ORDER:
        if n == 0:
            w_sib.start()
        for i in range(2):
            pl.when(2 * k + i != y)(lambda i=i, n=n: direct(i, n, True).start())
            pl.when(2 * k + i == y)(lambda i=i, n=n: direct(i, n, False).start())

    windows = ((k_win, r_k), (v_win, r_v))
    plan = (
        (3, 0, 1, sibling, None),
        (3, 1, 5, dev(z_o, y, 1 - k), has_out),
        (4, 2, 2, sibling, None),
        (4, 3, 0, dev(z_i, y, k), has_in),
        (4, 4, 6, dev(z_o, y, 1 - k), has_out),
        (2, 5, 0, sibling, has_out),
    )

    def forward(n, b, a, target, j):
        win, sems = windows[j]
        return pltpu.make_async_remote_copy(
            win.at[slot(a)], win.at[slot(b)], s_fwd.at[j, n], sems.at[slot(b)],
            device_id=target, device_id_type=MESH,
        )

    def arrived(sems, win, s):
        pltpu.make_async_copy(win.at[s], win.at[s], sems.at[s]).wait()

    def take(a, j):
        arrived(windows[j][1], windows[j][0], slot(a))
        for source, n, b, target, there in plan:
            if source != a:
                continue
            if there is None or a == 2:
                forward(n, b, a, target, j).start()
            else:
                pl.when(there)(lambda: forward(n, b, a, target, j).start())

    def lanes(s):
        return pl.ds(pl.multiple_of(s * TILE, TILE), TILE)

    def scores(i, s):
        raw = lax.dot_general(
            q_win[i], k_win[s], (((1,), (1,)), ((), ())), preferred_element_type=jnp.float32
        )
        score[i, :, lanes(s)] = raw
        high = jnp.maximum(jnp.maximum(raw[:, :HD], raw[:, HD : 2 * HD]), raw[:, 2 * HD :])
        m_ref[i] = jnp.maximum(m_ref[i], high - bias_win[i, pl.ds(s - i, 1), :])

    def weigh(i, j):
        off = m_ref[i][:, :1] + bias_win[i, pl.ds(j, 1), :][:, :1]
        exact = jnp.exp2((score[i, :, lanes(i + j)] - off) * FACTOR)
        weight[i, :, lanes(i + j)] = exact.astype(jnp.bfloat16)
        l_ref[i] = l_ref[i] + (exact[:, :HD] + exact[:, HD : 2 * HD] + exact[:, 2 * HD :])

    def product(i, s):
        acc_ref[i] = acc_ref[i] + jnp.dot(
            weight[i, :, lanes(s)], v_win[s], preferred_element_type=jnp.float32
        )

    def mirrored(i):
        return i + k * (1 - 2 * i)

    take(3, 0)
    take(4, 0)
    for i in range(2):
        arrived(r_q, q_win, i)
        arrived(r_b, bias_win, i)

    def near_scores(j, carry):
        s = slot(3 + j)

        @pl.when(j >= 2)
        def _():
            arrived(r_k, k_win, s)

        scores(0, s)
        scores(1, s)
        return carry

    lax.fori_loop(0, 4, near_scores, 0)

    @pl.when(has_out)
    def _():
        take(2, 0)
        arrived(r_k, k_win, slot(1))

    def far_scores(j, carry):
        s = slot(2 - j)
        scores(0, s)
        scores(1, s)
        return carry

    lax.fori_loop(0, 2, far_scores, 0)

    @pl.when(has_out)
    def _():
        arrived(r_k, k_win, slot(0))

    @pl.when(has_in)
    def _():
        arrived(r_k, k_win, slot(7))

    def last_scores(j, carry):
        scores(mirrored(j), slot(7 * j))
        return carry

    lax.fori_loop(0, 2, last_scores, 0)

    take(3, 1)
    take(4, 1)
    for i in range(2):
        m_ref[i] = jnp.broadcast_to(jnp.max(m_ref[i], axis=1, keepdims=True), (TILE, HD))

    def weigh_both(j, carry):
        weigh(0, j)
        weigh(1, j)
        return carry

    lax.fori_loop(0, 3, weigh_both, 0)
    lax.fori_loop(3, 7, weigh_both, 0)

    arrived(r_v, v_win, slot(5))
    arrived(r_v, v_win, slot(6))
    first = 3 - 2 * k
    own = pl.ds(pl.multiple_of(first * TILE, TILE), ROW * TILE)
    near_v = v_win[pl.ds(first, ROW)].reshape(ROW * TILE, HD)
    for i in range(2):
        acc_ref[i] = jnp.dot(weight[i, :, own], near_v, preferred_element_type=jnp.float32)

    @pl.when(has_out)
    def _():
        take(2, 1)
        arrived(r_v, v_win, slot(1))

    def far_products(j, carry):
        s = slot(2 - j)
        product(0, s)
        product(1, s)
        return carry

    lax.fori_loop(0, 2, far_products, 0)

    @pl.when(has_out)
    def _():
        arrived(r_v, v_win, slot(0))

    @pl.when(has_in)
    def _():
        arrived(r_v, v_win, slot(7))

    def last_products(j, carry):
        product(mirrored(j), slot(7 * j))
        return carry

    lax.fori_loop(0, 2, last_products, 0)

    def side(p):
        return (1 - yh) + p * (2 * yh - 1)

    def home(p, i, r, remote):
        src, dst = o_buf.at[i, r, side(p)], att.at[p, y]
        if remote:
            return pltpu.make_async_remote_copy(
                src, dst, s_o.at[p, i, r], r_o.at[p, y],
                device_id=dev(z, 2 * k + i, r), device_id_type=MESH,
            )
        return pltpu.make_async_copy(src, dst, r_o.at[p, y])

    for i in range(2):
        mixed = acc_ref[i] * (1.0 / jnp.sum(l_ref[i], axis=1, keepdims=True))
        for r in range(2):
            for h in range(2):
                first_rows = [OWN * (8 * h + 2 * xx + r) for xx in range(NX)]
                pieces = [mixed[at : at + OWN] for at in first_rows]
                o_buf[i, r, h] = jnp.concatenate(pieces, axis=0).astype(jnp.bfloat16)
    for p in range(2):
        for i in range(2):
            for r in range(2):
                here = (2 * k + i == y) & (k == r)
                pl.when(jnp.logical_not(here))(lambda: home(p, i, r, True).start())
                pl.when(here)(lambda: home(p, i, r, False).start())

    for n in ORDER:
        for i in range(2):
            pl.when(2 * k + i != y)(lambda i=i, n=n: direct(i, n, True).wait_send())
    for a, n, b, target, there in plan:
        for j in range(2):
            if there is None:
                forward(n, b, a, target, j).wait_send()
            else:
                pl.when(there)(lambda: forward(n, b, a, target, j).wait_send())
    w_sib.wait_send()
    w_own.wait()
    pltpu.make_async_copy(w_buf.at[1 - k], w_buf.at[1 - k], r_w.at[1 - k]).wait()

    chunks = []
    for p in range(2):
        start = 0
        for width in WIDTHS:
            chunks.append((p, slice(start, start + width)))
            start += width

    def toward(c):
        ahead = (x + 1 + 2 * ((c + k) % 2)) % NX
        return ahead, (ahead + 2) % NX

    def send(src, dst, s_sem, r_sem, target):
        return pltpu.make_async_remote_copy(
            src, dst, s_sem, r_sem, device_id=target, device_id_type=MESH
        )

    far = (x + 2) % NX

    def copy1(c):
        p, cols = chunks[c]
        return send(
            part.at[p, far, :, cols], got1.at[p, :, cols], s1, r1.at[c], xdev(toward(c)[0])
        )

    def copy2(c):
        p, cols = chunks[c]
        behind = toward(c)[1]
        return send(
            part.at[p, behind, :, cols], got2.at[p, :, cols], s2, r2.at[c], xdev(behind)
        )

    def copy3(c):
        p, cols = chunks[c]
        return send(
            send3.at[p, :, cols], got3.at[p, :, cols], s3, r3.at[c], xdev(toward(c)[0])
        )

    def copy4(cols, n):
        return send(send4.at[:, cols], got4.at[:, cols], s4, r4.at[n], partner)

    inputs = []

    def stage1(c):
        p, cols = chunks[c]
        if cols.start == 0:
            for j in range(ROW):
                pltpu.make_async_copy(att.at[p, j], att.at[p, j], r_o.at[p, j]).wait()
            inputs.append(
                [jnp.concatenate([att[p, j], att[p, j + 1]], axis=1) for j in (0, 2)]
            )
        low, high = inputs[p]
        total = jnp.dot(low, w_buf[0, :, cols], preferred_element_type=jnp.float32)
        total = total + jnp.dot(high, w_buf[1, :, cols], preferred_element_type=jnp.float32)
        width = cols.stop - cols.start
        part[p, :, :, cols] = total.reshape(NX, OWN, width).astype(jnp.bfloat16)
        copy1(c).start()
        copy2(c).start()

    def stage2(c):
        p, cols = chunks[c]
        copy1(c).wait_recv()
        own = part[p, toward(c)[0], :, cols].astype(jnp.float32)
        send3[p, :, cols] = (own + got1[p, :, cols].astype(jnp.float32)).astype(jnp.bfloat16)
        copy3(c).start()

    def stage3(c):
        p, cols = chunks[c]
        copy2(c).wait_recv()
        copy3(c).wait_recv()
        total = part[p, x, :, cols].astype(jnp.float32) + got2[p, :, cols].astype(jnp.float32)
        total = total + got3[p, :, cols].astype(jnp.float32)
        if p == 0:
            send4[:, cols] = total.astype(jnp.bfloat16)
            copy4(cols, c).start()
        else:
            copy4(cols, c - len(WIDTHS)).wait_recv()
            total = total + got4[:, cols].astype(jnp.float32)
            out_ref[:, cols] = total.astype(jnp.bfloat16)

    for step in range(len(chunks) + LAG3):
        for lag, stage in ((0, stage1), (LAG2, stage2), (LAG3, stage3)):
            if 0 <= step - lag < len(chunks):
                stage(step - lag)

    for p in range(2):
        for i in range(2):
            for r in range(2):
                here = (2 * k + i == y) & (k == r)
                pl.when(jnp.logical_not(here))(lambda: home(p, i, r, True).wait_send())
    for landed, sem in ((got1, s1), (got2, s2), (got3, s3), (got4, s4)):
        pltpu.make_async_copy(landed, landed, sem).wait()


def local(queries, keys, values, out_weight, neighbours, counts):
    bf16, f32 = jnp.bfloat16, jnp.float32
    vmem, dma = pltpu.VMEM, pltpu.SemaphoreType.DMA
    window = vmem((8, TILE, HD), bf16)
    per_query = vmem((2, TILE, HD), f32)
    ring = vmem((2, OWN, D), bf16)
    owned = vmem((OWN, D), bf16)
    chunks = 2 * len(WIDTHS)
    anywhere = pl.BlockSpec(memory_space=pltpu.HBM)
    operands = (queries, keys, values, out_weight, neighbours)
    return pl.pallas_call(
        body,
        out_shape=jax.ShapeDtypeStruct((OWN, D), bf16),
        in_specs=[anywhere] * 5 + [pl.BlockSpec(memory_space=pltpu.SMEM)],
        out_specs=pl.BlockSpec(memory_space=vmem),
        scratch_shapes=[
            pltpu.SMEM((1, 7), jnp.int32),
            vmem((2, TILE, HD), bf16), window, window,
            vmem((8, HD), f32), vmem((2, 8, HD), f32),
            vmem((2, TILE, 8 * TILE), f32), vmem((2, TILE, 8 * TILE), bf16),
            per_query, per_query, per_query,
            vmem((2, 2, 2, HALF, HD), bf16), vmem((2, ROW, HALF, HD), bf16),
            vmem((2, 2 * HD, D), bf16),
            vmem((2, NX, OWN, D), bf16), ring, ring, ring, ring, owned, owned,
            dma((2, 4)), dma((2,)), dma((8,)), dma((8,)), dma((2,)), dma((2, 6)),
            dma((2, 2, 2)), dma((2, ROW)), dma, dma((2,)), dma,
        ] + [dma] * 4 + [dma((chunks,))] * 4,
        compiler_params=pltpu.CompilerParams(
            collective_id=0, has_side_effects=True, vmem_limit_bytes=48 << 20
        ),
        name="tile_attention",
    )(*[pltpu.with_memory_space_constraint(a, pltpu.HBM) for a in operands], counts)


def solution(mesh):
    placed = (
        P("ctx", "head"),
        P("ctx", "head"),
        P("ctx", "head"),
        P("head", None),
        P("ctx", None),
        P("ctx"),
    )
    return jax.shard_map(
        local, mesh=mesh, in_specs=placed, out_specs=P(("ctx", "head"), None), check_vma=False
    )
```
